768 devices in a mesh: space: 48 (over z, x_lo, core), date: 8 (over y), head: 2 (over x_hi).
Axes of the slice: x: 4 (x_hi: 2, x_lo: 2; x = x_hi * 2 + x_lo), y: 8, z: 12, core: 2. Of those that a mesh axis runs over, the one named last changes fastest.
Arguments:
- latent_queries: bfloat16 [24576, 1536], P('space', 'head'), may hold values from -6 to 6
- grad_attention: bfloat16 [24576, 1536], P('space', 'head'), may hold values from -48 to 48
- cond_tokens: bfloat16 [3072, 1536], P('date'), may hold values from -6 to 6
- w_key: bfloat16 [1536, 1536], P(None, 'head'), may hold values from -0.15625 to 0.15625
- w_value: bfloat16 [1536, 1536], P(None, 'head'), may hold values from -0.15625 to 0.15625
- clear_tokens: int32 [48, 3072], P('space', 'date'), may hold values from 0 to 1, as said below
Outputs:
- grad_queries: bfloat16 [24576, 1536], P(('space', 'date'), 'head')
- grad_cond: bfloat16 [3072, 1536], P('date', ('space', 'head'))
The draws below stay inside these ranges and needn't reach their ends.
Inputs may be any that keep to these rules, and one draw needn't show every extreme that they name: `clear_tokens`: every tile has at least one clear condition token.
All inputs are finite; a program needn't handle non-finite values.
Results may differ from the reference program's by a relative error of at most 0.024.
Values may be sent and summed in bfloat16 or wider, within the bound.
No kernel may reach another device: no remote copies, remote signals or barrier semaphores. Data moves between devices by JAX's collectives and lax.ppermute only.
A program may use at most 64 MiB of HBM per device.

```python
import jax
import jax.numpy as jnp
from jax import lax

D = 1536
HEADS = 24
DH = 64
CPD = 48
LAT_DEV = 512
DATES = 64
COND = 3072
TILES = 48
LAT = 24576


def draw_clear_tokens(key, part):
    level_key, roll_key, pick_key = jax.random.split(key, 3)
    levels = jax.random.randint(level_key, (1, DATES), 1, 8)
    per_token = jnp.repeat(levels, CPD, axis=1)
    rolls = jax.random.randint(roll_key, (TILES, COND), 0, 8)
    forced = jax.random.randint(pick_key, (TILES, 1), 0, COND)
    positions = lax.broadcasted_iota(jnp.int32, (TILES, COND), 1)
    clear = (rolls < per_token) | (positions == forced)
    return clear.astype(jnp.int32)


def steps_of(rng, dims, cuts, smallest, largest):
    def one(axis_at, parts):
        steps = jax.random.uniform(jax.random.fold_in(jax.random.fold_in(rng, 6), axis_at), (parts,), jnp.float32, smallest / len(cuts), largest / len(cuts))
        return jnp.repeat(jnp.exp(steps), dims[axis_at] // parts).reshape((-1,) + (1,) * (len(dims) - axis_at - 1))

    loudness = one(*cuts[0])
    for cut in cuts[1:]:
        loudness = loudness * one(*cut)
    return loudness


def gaussian(own_key, dims, scale, bound, shards=(), dtype=jnp.bfloat16):
    array = scale * jax.random.normal(own_key, dims, jnp.float32)
    if shards:
        array = array * steps_of(own_key, dims, shards, -0.22, 0.18)
    return jnp.clip(array, -bound, bound).astype(dtype)


def setup_inputs(seed: int = 0) -> dict:
    splits = jax.random.split(jax.random.key(seed), 7)
    latent_queries = gaussian(splits[0], (LAT, D), 1.0, 6.0, ((0, 48), (1, 2)))
    grad_attention = gaussian(splits[1], (LAT, D), 8.0, 48.0, ((0, 48), (1, 2)))
    cond_tokens = gaussian(splits[2], (COND, D), 1.0, 6.0, ((0, 8),))
    w_key = gaussian(splits[3], (D, D), D ** -0.5, 0.15625, ((1, 2),))
    w_value = gaussian(splits[4], (D, D), D ** -0.5, 0.15625, ((1, 2),))
    clear_tokens = draw_clear_tokens(jax.random.fold_in(splits[6], 71), 0)
    return {"latent_queries": latent_queries, "grad_attention": grad_attention, "cond_tokens": cond_tokens, "w_key": w_key, "w_value": w_value, "clear_tokens": clear_tokens}


NORM_EPSILON = 1e-06

def unit_rms(values):
    return values * lax.rsqrt(lax.optimization_barrier(jnp.mean(values * values, axis=-1, keepdims=True)) + NORM_EPSILON)

def unit_rms_back(values, upstream):
    factor = lax.rsqrt(lax.optimization_barrier(jnp.mean(values * values, axis=-1, keepdims=True)) + NORM_EPSILON)
    normed = values * factor
    return factor * (upstream - normed * lax.optimization_barrier(jnp.mean(upstream * normed, axis=-1, keepdims=True)))

def reference(latent_queries, grad_attention, cond_tokens, w_key, w_value, clear_tokens):
    lat_rows = latent_queries.shape[0]
    cond_rows = cond_tokens.shape[0]
    score_scale = DH ** (-0.5)
    q_float = latent_queries.astype(jnp.float32).reshape(lat_rows, HEADS, DH)
    q_unit = unit_rms(q_float).astype(jnp.bfloat16)
    key_raw = jnp.dot(cond_tokens, w_key, preferred_element_type=jnp.float32).reshape(cond_rows, HEADS, DH)
    key_unit = unit_rms(key_raw).astype(jnp.bfloat16)
    value_rows = jnp.dot(cond_tokens, w_value, preferred_element_type=jnp.float32).astype(jnp.bfloat16).reshape(cond_rows, HEADS, DH)
    upstream = grad_attention.reshape(lat_rows, HEADS, DH)
    clear_mask = clear_tokens.astype(jnp.float32)

    def per_head(operands):
        query_head, key_head, value_head, grad_head = operands
        scores = jnp.dot(query_head, key_head.T, preferred_element_type=jnp.float32) * score_scale
        weights = (jnp.exp(scores).reshape(TILES, LAT_DEV, cond_rows) * clear_mask[:, None, :]).reshape(lat_rows, cond_rows)
        dprob = jnp.dot(grad_head, value_head.T, preferred_element_type=jnp.float32)
        total = lax.optimization_barrier(jnp.sum(weights, axis=1, keepdims=True))
        carried = lax.optimization_barrier(jnp.sum(weights * dprob, axis=1, keepdims=True))
        prob_float = weights / total
        prob = prob_float.astype(jnp.bfloat16)
        dscore = (prob_float * (dprob - carried / total)).astype(jnp.bfloat16)
        grad_values = jnp.dot(prob.T, grad_head, preferred_element_type=jnp.float32)
        grad_key_unit = jnp.dot(dscore.T, query_head, preferred_element_type=jnp.float32) * score_scale
        grad_q_unit = jnp.dot(dscore, key_head, preferred_element_type=jnp.float32) * score_scale
        return (grad_q_unit, grad_key_unit, grad_values)
    grad_q_unit, grad_key_unit, grad_values = lax.map(per_head, (q_unit.transpose(1, 0, 2), key_unit.transpose(1, 0, 2), value_rows.transpose(1, 0, 2), upstream.transpose(1, 0, 2)))
    grad_queries = unit_rms_back(q_float, grad_q_unit.transpose(1, 0, 2)).astype(jnp.bfloat16).reshape(lat_rows, HEADS * DH)
    grad_key_raw = unit_rms_back(key_raw, grad_key_unit.transpose(1, 0, 2)).astype(jnp.bfloat16).reshape(cond_rows, HEADS * DH)
    grad_value_rows = grad_values.transpose(1, 0, 2).reshape(cond_rows, HEADS * DH).astype(jnp.bfloat16)
    grad_cond = (jnp.dot(grad_key_raw, w_key.T, preferred_element_type=jnp.float32) + jnp.dot(grad_value_rows, w_value.T, preferred_element_type=jnp.float32)).astype(jnp.bfloat16)
    return (grad_queries, grad_cond)
```

```python
import jax
import jax.numpy as jnp
from jax import lax
from jax.experimental import pallas as pl
from jax.experimental.pallas import tpu as pltpu
from jax.sharding import Mesh, PartitionSpec as P

DH = 64
PAIR = 2 * DH
SPACE = ("z", "x", "core")
NEAR = ("x", "core", "head")

NORM_EPSILON = 1e-06

NT = (((1,), (1,)), ((), ()))
NN = (((1,), (0,)), ((), ()))


def dot(a, b, dims=NN):
    return lax.dot_general(a, b, dims, preferred_element_type=jnp.float32)


def head_mean(x, ones):
    high = x.astype(jnp.bfloat16)
    low = (x - high.astype(jnp.float32)).astype(jnp.bfloat16)
    return dot(jnp.concatenate([high, low], axis=1), ones) * (1.0 / DH)


def ones_of_heads():
    row = lax.broadcasted_iota(jnp.int32, (2 * PAIR, PAIR), 0) % PAIR
    column = lax.broadcasted_iota(jnp.int32, (2 * PAIR, PAIR), 1)
    return ((row < DH) == (column < DH)).astype(jnp.bfloat16)


def split_heads(x):
    lane = lax.broadcasted_iota(jnp.int32, x.shape, 1)
    zero = jnp.zeros_like(x)
    return jnp.concatenate([jnp.where(lane < DH, x, zero), jnp.where(lane < DH, zero, x)], axis=0)


def scores_kernel(q_ref, g_ref, cond_ref, wk_ref, wv_ref, mask_ref, w_ref, e_ref, sums_ref, keys_ref):
    cond_rows = cond_ref.shape[0]
    ones = ones_of_heads()
    projected = dot(cond_ref[...], jnp.concatenate([wk_ref[...], wv_ref[...]], axis=1))
    key_raw = projected[:, :PAIR]
    keys_ref[...] = key_raw
    key_unit = (key_raw * lax.rsqrt(head_mean(key_raw * key_raw, ones) + NORM_EPSILON)).astype(jnp.bfloat16)
    values = projected[:, PAIR:].astype(jnp.bfloat16)
    q = q_ref[...].astype(jnp.float32)
    q_unit = (q * lax.rsqrt(head_mean(q * q, ones) + NORM_EPSILON)).astype(jnp.bfloat16)
    scores = dot(split_heads(key_unit), q_unit, NT) * (DH ** -0.5)
    dprob = dot(split_heads(values), g_ref[...], NT)
    mask = mask_ref[...]
    sums = []
    for head in range(2):
        own = slice(head * cond_rows, (head + 1) * cond_rows)
        weights = jnp.exp(scores[own]) * mask
        carried = weights * dprob[own]
        w_ref[head] = weights.astype(jnp.bfloat16)
        e_ref[head] = carried.astype(jnp.bfloat16)
        sums += [jnp.sum(weights, axis=0, keepdims=True), jnp.sum(carried, axis=0, keepdims=True)]
    sums_ref[...] = jnp.broadcast_to(
        jnp.concatenate(sums, axis=0).astype(sums_ref.dtype)[None, None], sums_ref.shape
    )


def grads_kernel(q_ref, g_ref, keys_ref, wk_ref, wv_ref, w_ref, e_ref, sums_ref, gq_ref, gc_ref, acc_ref):
    cond_rows = keys_ref.shape[0]
    ones = ones_of_heads()
    q = q_ref[...].astype(jnp.float32)
    q_factor = lax.rsqrt(head_mean(q * q, ones) + NORM_EPSILON)
    q_normed = q * q_factor
    q_unit = q_normed.astype(jnp.bfloat16)
    key_raw = keys_ref[...]
    key_factor = lax.rsqrt(head_mean(key_raw * key_raw, ones) + NORM_EPSILON)
    key_normed = key_raw * key_factor
    keys_turned = key_normed.T.astype(jnp.bfloat16)
    g = g_ref[...]
    grad_values = []
    grad_keys = []
    grad_q = []
    sums = jnp.sum(sums_ref[:, 0].astype(jnp.float32), axis=0)
    for head in range(2):
        total = sums[2 * head : 2 * head + 1, :]
        carried = sums[2 * head + 1 : 2 * head + 2, :]
        inverse = 1.0 / total
        mean = carried * inverse
        weights = w_ref[head].astype(jnp.float32)
        prob = (weights * inverse).astype(jnp.bfloat16)
        dscore = ((e_ref[head].astype(jnp.float32) - weights * mean) * inverse).astype(jnp.bfloat16)
        grad_values.append(dot(prob, g))
        grad_keys.append(dot(dscore, q_unit))
        grad_q.append(dot(keys_turned[head * DH : (head + 1) * DH], dscore))
    lane = lax.broadcasted_iota(jnp.int32, (cond_rows, PAIR), 1)
    gv = jnp.where(lane < DH, grad_values[0], grad_values[1])
    gk = jnp.where(lane < DH, grad_keys[0], grad_keys[1]) * (DH ** -0.5)
    gq = jnp.concatenate(grad_q, axis=0).T * (DH ** -0.5)
    gq_back = q_factor * (gq - q_normed * head_mean(gq * q_normed, ones))
    gq_ref[...] = gq_back.astype(gq_ref.dtype)
    gk_back = key_factor * (gk - key_normed * head_mean(gk * key_normed, ones))
    both = jnp.concatenate([gk_back.astype(jnp.bfloat16), gv.astype(jnp.bfloat16)], axis=1)
    part = dot(jnp.concatenate([wk_ref[...], wv_ref[...]], axis=1), both, NT)
    step = pl.program_id(0)

    @pl.when(step == 0)
    def _():
        acc_ref[...] = part

    @pl.when(step > 0)
    def _():
        acc_ref[...] += part

    @pl.when(step == pl.num_programs(0) - 1)
    def _():
        near, far, own = gc_ref.shape[:3]
        for i in range(far):
            for j in range(near):
                start = (i * near + j) * own
                gc_ref[j, i] = acc_ref[start : start + own, :].astype(gc_ref.dtype)


def columns(rows):
    return pl.BlockSpec((rows, PAIR), lambda i: (0, i))


def whole(shape):
    return pl.BlockSpec(shape, lambda i: (0,) * len(shape), pipeline_mode=pl.Buffered(1))


def body(latent_queries, grad_attention, cond_tokens, w_key, w_value, clear_tokens):
    lat_rows, local_width = latent_queries.shape
    cond_rows, width = cond_tokens.shape
    pairs = local_width // PAIR
    mask = clear_tokens.astype(jnp.float32).reshape(cond_rows, 1)
    params = pltpu.CompilerParams(
        dimension_semantics=("arbitrary",), vmem_limit_bytes=56 * 1024 * 1024
    )
    score_block = pl.BlockSpec((2, cond_rows, lat_rows), lambda i: (i, 0, 0))
    dates = lax.axis_size("date")
    far = lax.axis_size("z")
    near = lax.axis_size(NEAR)
    own = width // (far * near)
    sums_block = pl.BlockSpec((dates, 1, 4, lat_rows), lambda i: (0, i, 0, 0))
    weights, carried, sums, key_raw = pl.pallas_call(
        scores_kernel,
        grid=(pairs,),
        in_specs=[
            columns(lat_rows),
            columns(lat_rows),
            whole((cond_rows, width)),
            columns(width),
            columns(width),
            whole((cond_rows, 1)),
        ],
        out_specs=[score_block, score_block, sums_block, columns(cond_rows)],
        out_shape=[
            jax.ShapeDtypeStruct((2 * pairs, cond_rows, lat_rows), jnp.bfloat16),
            jax.ShapeDtypeStruct((2 * pairs, cond_rows, lat_rows), jnp.bfloat16),
            jax.ShapeDtypeStruct((dates, pairs, 4, lat_rows), jnp.bfloat16),
            jax.ShapeDtypeStruct((cond_rows, local_width), jnp.float32),
        ],
        compiler_params=params,
        name="scores",
    )(latent_queries, grad_attention, cond_tokens, w_key, w_value, mask)
    sums = lax.all_to_all(sums, "date", 0, 0, tiled=True)
    grad_q, grad_c = pl.pallas_call(
        grads_kernel,
        grid=(pairs,),
        in_specs=[
            columns(lat_rows),
            columns(lat_rows),
            columns(cond_rows),
            columns(width),
            columns(width),
            score_block,
            score_block,
            sums_block,
        ],
        out_specs=[columns(lat_rows), whole((near, far, own, cond_rows))],
        out_shape=[
            jax.ShapeDtypeStruct((lat_rows, local_width), jnp.bfloat16),
            jax.ShapeDtypeStruct((near, far, own, cond_rows), jnp.bfloat16),
        ],
        scratch_shapes=[pltpu.VMEM((width, cond_rows), jnp.float32)],
        compiler_params=params,
        name="grads",
    )(latent_queries, grad_attention, key_raw, w_key, w_value, weights, carried, sums)
    grad_queries = lax.psum_scatter(grad_q, "date", scatter_dimension=0, tiled=True)
    near_parts = lax.all_to_all(grad_c, NEAR, 0, 0, tiled=True)
    near_sum = jnp.sum(near_parts.astype(jnp.float32), axis=0).astype(jnp.bfloat16)
    far_parts = lax.all_to_all(near_sum, "z", 0, 0, tiled=True)
    grad_cond = jnp.sum(far_parts.astype(jnp.float32), axis=0)
    return (grad_queries, grad_cond.T.astype(jnp.bfloat16))


def solution(mesh):
    space, dates, heads = mesh.devices.shape
    split = Mesh(
        mesh.devices.reshape(space // 4, 2, 2, dates, heads), ("z", "x", "core", "date", "head")
    )
    return jax.shard_map(
        body,
        mesh=split,
        in_specs=(
            P(SPACE, "head"),
            P(SPACE, "head"),
            P("date", None),
            P(None, "head"),
            P(None, "head"),
            P(SPACE, "date"),
        ),
        out_specs=(P(SPACE + ("date",), "head"), P("date", SPACE + ("head",))),
        check_vma=False,
    )
```

```python
import jax
import jax.numpy as jnp
from jax import lax
from jax.experimental import pallas as pl
from jax.experimental.pallas import tpu as pltpu
from jax.sharding import Mesh, PartitionSpec as P

DH = 64
PAIR = 2 * DH
SPACE = ("z", "x", "core")
CHIPS = ("x", "head")

NORM_EPSILON = 1e-06

NT = (((1,), (1,)), ((), ()))
NN = (((1,), (0,)), ((), ()))


def dot(a, b, dims=NN):
    return lax.dot_general(a, b, dims, preferred_element_type=jnp.float32)


def head_mean(x, ones):
    high = x.astype(jnp.bfloat16)
    low = (x - high.astype(jnp.float32)).astype(jnp.bfloat16)
    return dot(jnp.concatenate([high, low], axis=1), ones) * (1.0 / DH)


def ones_of_heads():
    row = lax.broadcasted_iota(jnp.int32, (2 * PAIR, PAIR), 0) % PAIR
    column = lax.broadcasted_iota(jnp.int32, (2 * PAIR, PAIR), 1)
    return ((row < DH) == (column < DH)).astype(jnp.bfloat16)


def split_heads(x):
    lane = lax.broadcasted_iota(jnp.int32, x.shape, 1)
    zero = jnp.zeros_like(x)
    return jnp.concatenate([jnp.where(lane < DH, x, zero), jnp.where(lane < DH, zero, x)], axis=0)


def scores_kernel(q_ref, g_ref, cond_ref, wk_ref, wv_ref, clear_ref, w_ref, e_ref, sums_ref, keys_ref, mask_ref):
    cond_rows = cond_ref.shape[0]
    lat_rows = q_ref.shape[0]

    @pl.when(pl.program_id(0) == 0)
    def _():
        mask_ref[...] = jnp.broadcast_to(clear_ref[...].astype(jnp.float32), (PAIR, cond_rows)).T

    ones = ones_of_heads()
    projected = dot(cond_ref[...], jnp.concatenate([wk_ref[...], wv_ref[...]], axis=1))
    key_raw = projected[:, :PAIR]
    keys_ref[...] = key_raw
    key_unit = (key_raw * lax.rsqrt(head_mean(key_raw * key_raw, ones) + NORM_EPSILON)).astype(jnp.bfloat16)
    values = projected[:, PAIR:].astype(jnp.bfloat16)
    q = q_ref[...].astype(jnp.float32)
    q_unit = (q * lax.rsqrt(head_mean(q * q, ones) + NORM_EPSILON)).astype(jnp.bfloat16)
    scores = dot(split_heads(key_unit), q_unit, NT) * (DH ** -0.5)
    dprob = dot(split_heads(values), g_ref[...], NT)
    mask = jnp.concatenate([mask_ref[...]] * (lat_rows // PAIR), axis=1)
    sums = []
    for head in range(2):
        own = slice(head * cond_rows, (head + 1) * cond_rows)
        weights = jnp.exp(scores[own]) * mask
        carried = weights * dprob[own]
        w_ref[head] = weights.astype(jnp.bfloat16)
        e_ref[head] = carried.astype(jnp.bfloat16)
        sums += [jnp.sum(weights, axis=0, keepdims=True), jnp.sum(carried, axis=0, keepdims=True)]
    sums_ref[...] = jnp.broadcast_to(
        jnp.concatenate(sums, axis=0).astype(sums_ref.dtype)[None, None], sums_ref.shape
    )


def queries_kernel(keys_ref, w_ref, e_ref, plain_ref, carried_ref):
    ones = ones_of_heads()
    key_raw = keys_ref[...]
    key_unit = key_raw * lax.rsqrt(head_mean(key_raw * key_raw, ones) + NORM_EPSILON)
    turned = key_unit.T.astype(jnp.bfloat16)
    for head in range(2):
        own = turned[head * DH : (head + 1) * DH]
        plain_ref[head] = dot(own, w_ref[head])
        carried_ref[head] = dot(own, e_ref[head])


def grads_kernel(
    place_ref, q_ref, g_ref, keys_ref, wk_ref, wv_ref, w_ref, e_ref, plain_ref, carried_ref, sums_ref,
    gq_ref, keep_ref, send_ref, acc_ref
):
    cond_rows = keys_ref.shape[0]
    ones = ones_of_heads()
    q = q_ref[...].astype(jnp.float32)
    q_factor = lax.rsqrt(head_mean(q * q, ones) + NORM_EPSILON)
    q_normed = q * q_factor
    q_unit = q_normed.astype(jnp.bfloat16)
    key_raw = keys_ref[...]
    key_factor = lax.rsqrt(head_mean(key_raw * key_raw, ones) + NORM_EPSILON)
    key_normed = key_raw * key_factor
    g = g_ref[...]
    grad_values = []
    grad_keys = []
    grad_q = []
    sums = jnp.sum(sums_ref[:, pl.program_id(0)].astype(jnp.float32), axis=0)
    for head in range(2):
        total = sums[2 * head : 2 * head + 1, :]
        carried = sums[2 * head + 1 : 2 * head + 2, :]
        inverse = 1.0 / total
        mean = carried * inverse
        weights = w_ref[head].astype(jnp.float32)
        prob = (weights * inverse).astype(jnp.bfloat16)
        dscore = ((e_ref[head].astype(jnp.float32) - weights * mean) * inverse).astype(jnp.bfloat16)
        grad_values.append(dot(prob, g))
        grad_keys.append(dot(dscore, q_unit))
        grad_q.append((carried_ref[head] - plain_ref[head] * mean) * inverse)
    lane = lax.broadcasted_iota(jnp.int32, (cond_rows, PAIR), 1)
    gv = jnp.where(lane < DH, grad_values[0], grad_values[1])
    gk = jnp.where(lane < DH, grad_keys[0], grad_keys[1]) * (DH ** -0.5)
    gq = jnp.concatenate(grad_q, axis=0).T * (DH ** -0.5)
    gq_back = q_factor * (gq - q_normed * head_mean(gq * q_normed, ones))
    gq_ref[...] = gq_back.astype(gq_ref.dtype)
    gk_back = key_factor * (gk - key_normed * head_mean(gk * key_normed, ones))
    both = jnp.concatenate([gk_back.astype(jnp.bfloat16), gv.astype(jnp.bfloat16)], axis=1)
    part = dot(jnp.concatenate([wk_ref[...], wv_ref[...]], axis=1), both, NT)
    step = pl.program_id(0)

    @pl.when(step == 0)
    def _():
        acc_ref[...] = part

    @pl.when(step > 0)
    def _():
        acc_ref[...] += part

    @pl.when(step == pl.num_programs(0) - 1)
    def _():
        chips, far, own = keep_ref.shape[:3]
        x, core, head = place_ref[0], place_ref[1], place_ref[2]
        for chip in range(chips):
            to_x = x ^ (chip // 2)
            to_head = head ^ (chip % 2)
            for ref, to_core in ((keep_ref, core), (send_ref, core ^ 1)):
                near = (to_x * 2 + to_core) * 2 + to_head
                for i in range(far):
                    start = pl.multiple_of((i * 8 + near) * own, own)
                    ref[chip, i] = acc_ref[pl.ds(start, own), :].astype(ref.dtype)


def columns(rows):
    return pl.BlockSpec((rows, PAIR), lambda i: (0, i))


def whole(shape):
    return pl.BlockSpec(shape, lambda i: (0,) * len(shape), pipeline_mode=pl.Buffered(1))


def add(*parts):
    return sum(part.astype(jnp.float32) for part in parts).astype(jnp.bfloat16)


def body(latent_queries, grad_attention, cond_tokens, w_key, w_value, clear_tokens):
    lat_rows, local_width = latent_queries.shape
    cond_rows, width = cond_tokens.shape
    pairs = local_width // PAIR
    dates = lax.axis_size("date")
    far = lax.axis_size("z")
    chips = lax.axis_size(CHIPS)
    own = width // (far * chips * 2)
    params = pltpu.CompilerParams(
        dimension_semantics=("arbitrary",), vmem_limit_bytes=56 * 1024 * 1024
    )
    score_block = pl.BlockSpec((2, cond_rows, lat_rows), lambda i: (i, 0, 0))
    query_block = pl.BlockSpec((2, DH, lat_rows), lambda i: (i, 0, 0))
    sums_block = pl.BlockSpec((dates, 1, 4, lat_rows), lambda i: (0, i, 0, 0))
    score_shape = jax.ShapeDtypeStruct((2 * pairs, cond_rows, lat_rows), jnp.bfloat16)
    query_shape = jax.ShapeDtypeStruct((2 * pairs, DH, lat_rows), jnp.float32)
    piece_shape = jax.ShapeDtypeStruct((chips, far, own, cond_rows), jnp.bfloat16)
    weights, carried, sums, key_raw = pl.pallas_call(
        scores_kernel,
        grid=(pairs,),
        in_specs=[
            columns(lat_rows),
            columns(lat_rows),
            whole((cond_rows, width)),
            columns(width),
            columns(width),
            whole((1, cond_rows)),
        ],
        out_specs=[score_block, score_block, sums_block, columns(cond_rows)],
        out_shape=[
            score_shape,
            score_shape,
            jax.ShapeDtypeStruct((dates, pairs, 4, lat_rows), jnp.bfloat16),
            jax.ShapeDtypeStruct((cond_rows, local_width), jnp.float32),
        ],
        scratch_shapes=[pltpu.VMEM((cond_rows, PAIR), jnp.float32)],
        compiler_params=params,
        name="scores",
    )(latent_queries, grad_attention, cond_tokens, w_key, w_value, clear_tokens)
    sums = lax.all_to_all(sums, "date", 0, 0, tiled=True)
    plain_q, carried_q = pl.pallas_call(
        queries_kernel,
        grid=(pairs,),
        in_specs=[columns(cond_rows), score_block, score_block],
        out_specs=[query_block, query_block],
        out_shape=[query_shape, query_shape],
        compiler_params=params,
        name="queries",
    )(key_raw, weights, carried)
    place = jnp.stack([lax.axis_index("x"), lax.axis_index("core"), lax.axis_index("head")])
    grad_q, keep, send = pl.pallas_call(
        grads_kernel,
        grid=(pairs,),
        in_specs=[
            pl.BlockSpec(memory_space=pltpu.SMEM),
            columns(lat_rows),
            columns(lat_rows),
            columns(cond_rows),
            columns(width),
            columns(width),
            score_block,
            score_block,
            query_block,
            query_block,
            pl.BlockSpec(memory_space=pltpu.VMEM),
        ],
        out_specs=[columns(lat_rows), whole(piece_shape.shape), whole(piece_shape.shape)],
        out_shape=[
            jax.ShapeDtypeStruct((lat_rows, local_width), jnp.bfloat16),
            piece_shape,
            piece_shape,
        ],
        scratch_shapes=[pltpu.VMEM((width, cond_rows), jnp.float32)],
        compiler_params=params,
        name="grads",
    )(
        place, latent_queries, grad_attention, key_raw, w_key, w_value,
        weights, carried, plain_q, carried_q, sums,
    )
    share_parts = lax.all_to_all(
        grad_q.reshape(dates, lat_rows // dates, local_width), "date", 0, 0, tiled=True
    )
    other = lax.ppermute(send, "core", [(0, 1), (1, 0)])
    halves = [add(keep[chip], other[chip]) for chip in range(chips)]
    near_parts = halves[:1] + [
        lax.ppermute(halves[chip], CHIPS, [(i, i ^ chip) for i in range(chips)])
        for chip in range(1, chips)
    ]
    near_sum, share_parts = lax.optimization_barrier((add(*near_parts), share_parts))
    far_parts = lax.all_to_all(near_sum, "z", 0, 0, tiled=True)
    grad_queries = jnp.sum(share_parts.astype(jnp.float32), axis=0).astype(jnp.bfloat16)
    grad_cond = jnp.sum(far_parts.astype(jnp.float32), axis=0)
    return (grad_queries, grad_cond.T.astype(jnp.bfloat16))


def solution(mesh):
    space, dates, heads = mesh.devices.shape
    split = Mesh(
        mesh.devices.reshape(space // 4, 2, 2, dates, heads), ("z", "x", "core", "date", "head")
    )
    return jax.shard_map(
        body,
        mesh=split,
        in_specs=(
            P(SPACE, "head"),
            P(SPACE, "head"),
            P("date", None),
            P(None, "head"),
            P(None, "head"),
            P(SPACE, "date"),
        ),
        out_specs=(P(SPACE + ("date",), "head"), P("date", SPACE + ("head",))),
        check_vma=False,
    )
```

```python
import jax
import jax.numpy as jnp
from jax import lax
from jax.experimental import pallas as pl
from jax.experimental.pallas import tpu as pltpu
from jax.sharding import Mesh, PartitionSpec as P

DH = 64
PAIR = 2 * DH
STEP = 3
SPACE = ("z", "x", "core")
CHIPS = ("x", "head")

NORM_EPSILON = 1e-06

NT = (((1,), (1,)), ((), ()))
NN = (((1,), (0,)), ((), ()))


def dot(a, b, dims=NN):
    return lax.dot_general(a, b, dims, preferred_element_type=jnp.float32)


def head_mean(x):
    first = lax.broadcasted_iota(jnp.int32, x.shape, 1) < DH
    zero = jnp.zeros_like(x)
    left = jnp.sum(jnp.where(first, x, zero), axis=1, keepdims=True)
    right = jnp.sum(jnp.where(first, zero, x), axis=1, keepdims=True)
    return jnp.where(first, left, right) * (1.0 / DH)


def scores_kernel(
    q_ref, g_ref, cond_ref, wk_ref, wv_ref, clear_ref,
    w_ref, e_ref, sums_ref, keys_ref, mask_ref
):
    cond_rows = cond_ref.shape[0]
    lat_rows = q_ref.shape[0]

    @pl.when(pl.program_id(0) == 0)
    def _():
        mask_ref[...] = jnp.broadcast_to(clear_ref[...].astype(jnp.float32), (PAIR, cond_rows)).T

    for sub in range(STEP):
        lanes = slice(sub * PAIR, (sub + 1) * PAIR)
        projected = dot(
            cond_ref[...], jnp.concatenate([wk_ref[:, lanes], wv_ref[:, lanes]], axis=1)
        )
        key_raw = projected[:, :PAIR]
        keys_ref[:, lanes] = key_raw
        key_normed = key_raw * lax.rsqrt(head_mean(key_raw * key_raw) + NORM_EPSILON)
        key_unit = key_normed.astype(jnp.bfloat16)
        values = projected[:, PAIR:].astype(jnp.bfloat16)
        q = q_ref[:, lanes].astype(jnp.float32)
        q_unit = (q * lax.rsqrt(head_mean(q * q) + NORM_EPSILON)).astype(jnp.bfloat16)
        first = lax.broadcasted_iota(jnp.int32, key_unit.shape, 1) < DH
        nothing = jnp.zeros_like(key_unit)
        mask = jnp.concatenate([mask_ref[...]] * (lat_rows // PAIR), axis=1)
        sums = []
        for head in range(2):
            mine = first if head == 0 else ~first
            scores = dot(jnp.where(mine, key_unit, nothing), q_unit, NT) * (DH ** -0.5)
            dprob = dot(jnp.where(mine, values, nothing), g_ref[:, lanes], NT)
            weights = jnp.exp(scores) * mask
            carried = weights * dprob
            w_ref[2 * sub + head] = weights.astype(jnp.bfloat16)
            e_ref[2 * sub + head] = carried.astype(jnp.bfloat16)
            sums += [jnp.sum(weights, axis=0, keepdims=True), jnp.sum(carried, axis=0, keepdims=True)]
        sums = jnp.concatenate(sums, axis=0).astype(sums_ref.dtype)
        sums_ref[:, sub] = jnp.broadcast_to(sums[None], (sums_ref.shape[0],) + sums.shape)


def means_of(sums_ref, pair, head):
    sums = jnp.sum(sums_ref[:, pair, 2 * head : 2 * head + 2].astype(jnp.float32), axis=0)
    inverse = 1.0 / sums[:1]
    return inverse, sums[1:] * inverse


def grads_kernel(
    place_ref, q_ref, g_ref, keys_ref, wk_ref, wv_ref, w_ref, e_ref, sums_ref,
    gq_ref, keep_ref, send_ref, acc_ref
):
    cond_rows = keys_ref.shape[0]
    step = pl.program_id(0)
    both = []
    for sub in range(STEP):
        lanes = slice(sub * PAIR, (sub + 1) * PAIR)
        q = q_ref[:, lanes].astype(jnp.float32)
        q_factor = lax.rsqrt(head_mean(q * q) + NORM_EPSILON)
        q_normed = q * q_factor
        q_unit = q_normed.astype(jnp.bfloat16)
        key_raw = keys_ref[:, lanes]
        key_factor = lax.rsqrt(head_mean(key_raw * key_raw) + NORM_EPSILON)
        key_normed = key_raw * key_factor
        turned = key_normed.T.astype(jnp.bfloat16)
        probs = []
        dscores = []
        for head in range(2):
            inverse, mean = means_of(sums_ref, sub, head)
            weights = w_ref[2 * sub + head].astype(jnp.float32)
            probs.append((weights * inverse).astype(jnp.bfloat16))
            dscore = (e_ref[2 * sub + head].astype(jnp.float32) - weights * mean) * inverse
            dscores.append(dscore.astype(jnp.bfloat16))
        gq = [dot(turned[head * DH : (head + 1) * DH], dscores[head]) for head in range(2)]
        gq = jnp.concatenate(gq, axis=0).T * (DH ** -0.5)
        gq = q_factor * (gq - q_normed * head_mean(gq * q_normed))
        gq_ref[:, lanes] = gq.astype(gq_ref.dtype)
        lane = lax.broadcasted_iota(jnp.int32, (cond_rows, PAIR), 1)
        grad_values = dot(jnp.concatenate(probs, axis=0), g_ref[:, lanes])
        grad_keys = dot(jnp.concatenate(dscores, axis=0), q_unit)
        gv = jnp.where(lane < DH, grad_values[:cond_rows], grad_values[cond_rows:])
        gk = jnp.where(lane < DH, grad_keys[:cond_rows], grad_keys[cond_rows:]) * (DH ** -0.5)
        gk_back = key_factor * (gk - key_normed * head_mean(gk * key_normed))
        both += [gk_back.astype(jnp.bfloat16), gv.astype(jnp.bfloat16)]
    w_both = []
    for sub in range(STEP):
        lanes = slice(sub * PAIR, (sub + 1) * PAIR)
        w_both += [wk_ref[:, lanes], wv_ref[:, lanes]]
    part = dot(jnp.concatenate(w_both, axis=1), jnp.concatenate(both, axis=1), NT)

    @pl.when(step == 0)
    def _():
        acc_ref[...] = part

    @pl.when(step > 0)
    def _():
        acc_ref[...] += part

    @pl.when(step == pl.num_programs(0) - 1)
    def _():
        chips, far, own = keep_ref.shape[:3]
        x, core, head = place_ref[0], place_ref[1], place_ref[2]
        for chip in range(chips):
            to_x = x ^ (chip // 2)
            to_head = head ^ (chip % 2)
            for ref, to_core in ((keep_ref, core), (send_ref, core ^ 1)):
                near = (to_x * 2 + to_core) * 2 + to_head
                for i in range(far):
                    start = pl.multiple_of((i * 8 + near) * own, own)
                    ref[chip, i] = acc_ref[pl.ds(start, own), :].astype(ref.dtype)


def columns(rows):
    return pl.BlockSpec((rows, STEP * PAIR), lambda i: (0, i))


def whole(shape):
    return pl.BlockSpec(shape, lambda i: (0,) * len(shape), pipeline_mode=pl.Buffered(1))


def in_hbm(*arrays):
    return [pltpu.with_memory_space_constraint(array, pltpu.HBM) for array in arrays]


def add(*parts):
    return sum(part.astype(jnp.float32) for part in parts).astype(jnp.bfloat16)


def body(latent_queries, grad_attention, cond_tokens, w_key, w_value, clear_tokens):
    lat_rows, local_width = latent_queries.shape
    cond_rows, width = cond_tokens.shape
    pairs = local_width // PAIR
    latent_queries, grad_attention, cond_tokens, w_key, w_value = in_hbm(
        latent_queries, grad_attention, cond_tokens, w_key, w_value
    )
    dates = lax.axis_size("date")
    far = lax.axis_size("z")
    chips = lax.axis_size(CHIPS)
    own = width // (far * chips * 2)
    params = pltpu.CompilerParams(
        dimension_semantics=("arbitrary",), vmem_limit_bytes=36 * 1024 * 1024
    )
    score_block = pl.BlockSpec((2 * STEP, cond_rows, lat_rows), lambda i: (i, 0, 0))
    sums_block = pl.BlockSpec((dates, STEP, 4, lat_rows), lambda i: (0, i, 0, 0))
    score_shape = pltpu.HBM((2 * pairs, cond_rows, lat_rows), jnp.bfloat16)
    piece_shape = pltpu.HBM((chips, far, own, cond_rows), jnp.bfloat16)
    weights, carried, sums, key_raw = pl.pallas_call(
        scores_kernel,
        grid=(pairs // STEP,),
        in_specs=[
            columns(lat_rows),
            columns(lat_rows),
            whole((cond_rows, width)),
            columns(width),
            columns(width),
            whole((1, cond_rows)),
        ],
        out_specs=[score_block, score_block, sums_block, columns(cond_rows)],
        out_shape=[
            score_shape,
            score_shape,
            pltpu.HBM((dates, pairs, 4, lat_rows), jnp.bfloat16),
            pltpu.HBM((cond_rows, local_width), jnp.float32),
        ],
        scratch_shapes=[pltpu.VMEM((cond_rows, PAIR), jnp.float32)],
        compiler_params=params,
        name="scores",
    )(latent_queries, grad_attention, cond_tokens, w_key, w_value, clear_tokens)
    weights, carried, key_raw = in_hbm(weights, carried, key_raw)
    sums = lax.all_to_all(sums, "date", 0, 0, tiled=True)
    place = jnp.stack([lax.axis_index("x"), lax.axis_index("core"), lax.axis_index("head")])
    grad_q, keep, send = pl.pallas_call(
        grads_kernel,
        grid=(pairs // STEP,),
        in_specs=[
            pl.BlockSpec(memory_space=pltpu.SMEM),
            columns(lat_rows),
            columns(lat_rows),
            columns(cond_rows),
            columns(width),
            columns(width),
            score_block,
            score_block,
            sums_block,
        ],
        out_specs=[columns(lat_rows), whole(piece_shape.shape), whole(piece_shape.shape)],
        out_shape=[
            jax.ShapeDtypeStruct((lat_rows, local_width), jnp.bfloat16),
            piece_shape,
            piece_shape,
        ],
        scratch_shapes=[pltpu.VMEM((width, cond_rows), jnp.float32)],
        compiler_params=params,
        name="grads",
    )(place, latent_queries, grad_attention, key_raw, w_key, w_value, weights, carried, sums)
    share_parts = lax.all_to_all(
        grad_q.reshape(dates, lat_rows // dates, local_width), "date", 0, 0, tiled=True
    )
    other = lax.ppermute(send, "core", [(0, 1), (1, 0)])
    halves = [add(keep[chip], other[chip]) for chip in range(chips)]
    near_parts = halves[:1] + [
        lax.ppermute(halves[chip], CHIPS, [(i, i ^ chip) for i in range(chips)])
        for chip in range(1, chips)
    ]
    near_sum, share_parts = lax.optimization_barrier((add(*near_parts), share_parts))
    far_parts = lax.all_to_all(near_sum, "z", 0, 0, tiled=True)
    grad_queries = jnp.sum(share_parts.astype(jnp.float32), axis=0).astype(jnp.bfloat16)
    grad_cond = jnp.sum(far_parts.astype(jnp.float32), axis=0)
    return (grad_queries, grad_cond.T.astype(jnp.bfloat16))


def solution(mesh):
    space, dates, heads = mesh.devices.shape
    split = Mesh(
        mesh.devices.reshape(space // 4, 2, 2, dates, heads), ("z", "x", "core", "date", "head")
    )
    return jax.shard_map(
        body,
        mesh=split,
        in_specs=(
            P(SPACE, "head"),
            P(SPACE, "head"),
            P("date", None),
            P(None, "head"),
            P(None, "head"),
            P(SPACE, "date"),
        ),
        out_specs=(P(SPACE + ("date",), "head"), P("date", SPACE + ("head",))),
        check_vma=False,
    )
```

```python
import jax
import jax.numpy as jnp
from jax import lax
from jax.experimental import pallas as pl
from jax.experimental.pallas import tpu as pltpu
from jax.sharding import Mesh, PartitionSpec as P

DH = 64
PAIR = 2 * DH
STEP = 3
SPACE = ("z", "x", "core")
CHIPS = ("x", "head")

NORM_EPSILON = 1e-06

NT = (((1,), (1,)), ((), ()))
NN = (((1,), (0,)), ((), ()))


def dot(a, b, dims=NN):
    return lax.dot_general(a, b, dims, preferred_element_type=jnp.float32)


def head_mean(x):
    first = lax.broadcasted_iota(jnp.int32, x.shape, 1) < DH
    zero = jnp.zeros_like(x)
    left = jnp.sum(jnp.where(first, x, zero), axis=1, keepdims=True)
    right = jnp.sum(jnp.where(first, zero, x), axis=1, keepdims=True)
    return jnp.where(first, left, right) * (1.0 / DH)


def place_of(sub, head, w_ref, e_ref, w_near_ref, e_near_ref):
    if sub < STEP - 1:
        return w_ref, e_ref, 2 * sub + head
    return w_near_ref, e_near_ref, 2 * pl.program_id(0) + head


def scores_kernel(
    q_ref, g_ref, cond_ref, wk_ref, wv_ref, clear_ref,
    w_ref, e_ref, w_near_ref, e_near_ref, sums_ref, keys_ref, mask_ref
):
    cond_rows = cond_ref.shape[0]
    lat_rows = q_ref.shape[0]

    @pl.when(pl.program_id(0) == 0)
    def _():
        mask_ref[...] = jnp.broadcast_to(clear_ref[...].astype(jnp.float32), (PAIR, cond_rows)).T

    for sub in range(STEP):
        lanes = slice(sub * PAIR, (sub + 1) * PAIR)
        projected = dot(
            cond_ref[...], jnp.concatenate([wk_ref[:, lanes], wv_ref[:, lanes]], axis=1)
        )
        key_raw = projected[:, :PAIR]
        keys_ref[:, lanes] = key_raw
        key_normed = key_raw * lax.rsqrt(head_mean(key_raw * key_raw) + NORM_EPSILON)
        key_unit = key_normed.astype(jnp.bfloat16)
        values = projected[:, PAIR:].astype(jnp.bfloat16)
        q = q_ref[:, lanes].astype(jnp.float32)
        q_unit = (q * lax.rsqrt(head_mean(q * q) + NORM_EPSILON)).astype(jnp.bfloat16)
        first = lax.broadcasted_iota(jnp.int32, key_unit.shape, 1) < DH
        nothing = jnp.zeros_like(key_unit)
        mask = jnp.concatenate([mask_ref[...]] * (lat_rows // PAIR), axis=1)
        sums = []
        for head in range(2):
            mine = first if head == 0 else ~first
            scores = dot(jnp.where(mine, key_unit, nothing), q_unit, NT) * (DH ** -0.5)
            dprob = dot(jnp.where(mine, values, nothing), g_ref[:, lanes], NT)
            weights = jnp.exp(scores) * mask
            carried = weights * dprob
            own_w, own_e, at = place_of(sub, head, w_ref, e_ref, w_near_ref, e_near_ref)
            own_w[at] = weights.astype(jnp.bfloat16)
            own_e[at] = carried.astype(jnp.bfloat16)
            sums += [jnp.sum(weights, axis=0, keepdims=True), jnp.sum(carried, axis=0, keepdims=True)]
        sums = jnp.concatenate(sums, axis=0).astype(sums_ref.dtype)
        sums_ref[:, sub] = jnp.broadcast_to(sums[None], (sums_ref.shape[0],) + sums.shape)


def means_of(sums_ref, pair, head):
    sums = jnp.sum(sums_ref[:, pair, 2 * head : 2 * head + 2].astype(jnp.float32), axis=0)
    inverse = 1.0 / sums[:1]
    return inverse, sums[1:] * inverse


def grads_kernel(
    place_ref, q_ref, g_ref, keys_ref, wk_ref, wv_ref, w_ref, e_ref, w_near_ref, e_near_ref, sums_ref,
    gq_ref, keep_ref, send_ref, acc_ref
):
    cond_rows = keys_ref.shape[0]
    step = pl.program_id(0)
    both = []
    for sub in range(STEP):
        lanes = slice(sub * PAIR, (sub + 1) * PAIR)
        q = q_ref[:, lanes].astype(jnp.float32)
        q_factor = lax.rsqrt(head_mean(q * q) + NORM_EPSILON)
        q_normed = q * q_factor
        q_unit = q_normed.astype(jnp.bfloat16)
        key_raw = keys_ref[:, lanes]
        key_factor = lax.rsqrt(head_mean(key_raw * key_raw) + NORM_EPSILON)
        key_normed = key_raw * key_factor
        turned = key_normed.T.astype(jnp.bfloat16)
        probs = []
        dscores = []
        for head in range(2):
            inverse, mean = means_of(sums_ref, sub, head)
            own_w, own_e, at = place_of(sub, head, w_ref, e_ref, w_near_ref, e_near_ref)
            weights = own_w[at].astype(jnp.float32)
            probs.append((weights * inverse).astype(jnp.bfloat16))
            dscore = (own_e[at].astype(jnp.float32) - weights * mean) * inverse
            dscores.append(dscore.astype(jnp.bfloat16))
        gq = [dot(turned[head * DH : (head + 1) * DH], dscores[head]) for head in range(2)]
        gq = jnp.concatenate(gq, axis=0).T * (DH ** -0.5)
        gq = q_factor * (gq - q_normed * head_mean(gq * q_normed))
        gq_ref[:, :, lanes] = gq.astype(gq_ref.dtype).reshape(gq_ref.shape[:2] + (PAIR,))
        lane = lax.broadcasted_iota(jnp.int32, (cond_rows, PAIR), 1)
        grad_values = dot(jnp.concatenate(probs, axis=0), g_ref[:, lanes])
        grad_keys = dot(jnp.concatenate(dscores, axis=0), q_unit)
        gv = jnp.where(lane < DH, grad_values[:cond_rows], grad_values[cond_rows:])
        gk = jnp.where(lane < DH, grad_keys[:cond_rows], grad_keys[cond_rows:]) * (DH ** -0.5)
        gk_back = key_factor * (gk - key_normed * head_mean(gk * key_normed))
        both += [gk_back.astype(jnp.bfloat16), gv.astype(jnp.bfloat16)]
    w_both = []
    for sub in range(STEP):
        lanes = slice(sub * PAIR, (sub + 1) * PAIR)
        w_both += [wk_ref[:, lanes], wv_ref[:, lanes]]
    part = dot(jnp.concatenate(w_both, axis=1), jnp.concatenate(both, axis=1), NT)

    @pl.when(step == 0)
    def _():
        acc_ref[...] = part

    @pl.when(step > 0)
    def _():
        acc_ref[...] += part

    @pl.when(step == pl.num_programs(0) - 1)
    def _():
        chips, far, own = keep_ref.shape[:3]
        x, core, head = place_ref[0], place_ref[1], place_ref[2]
        for chip in range(chips):
            to_x = x ^ (chip // 2)
            to_head = head ^ (chip % 2)
            for ref, to_core in ((keep_ref, core), (send_ref, core ^ 1)):
                near = (to_x * 2 + to_core) * 2 + to_head
                for i in range(far):
                    start = pl.multiple_of((i * 8 + near) * own, own)
                    ref[chip, i] = acc_ref[pl.ds(start, own), :].astype(ref.dtype)


def columns(rows):
    return pl.BlockSpec((rows, STEP * PAIR), lambda i: (0, i))


def whole(shape):
    return pl.BlockSpec(shape, lambda i: (0,) * len(shape), pipeline_mode=pl.Buffered(1))


def in_hbm(*arrays):
    return [pltpu.with_memory_space_constraint(array, pltpu.HBM) for array in arrays]


def add(*parts):
    return sum(part.astype(jnp.float32) for part in parts).astype(jnp.bfloat16)


def body(latent_queries, grad_attention, cond_tokens, w_key, w_value, clear_tokens):
    lat_rows, local_width = latent_queries.shape
    cond_rows, width = cond_tokens.shape
    pairs = local_width // PAIR
    latent_queries, grad_attention, cond_tokens, w_key, w_value, clear_tokens = in_hbm(
        latent_queries, grad_attention, cond_tokens, w_key, w_value, clear_tokens
    )
    dates = lax.axis_size("date")
    far = lax.axis_size("z")
    chips = lax.axis_size(CHIPS)
    own = width // (far * chips * 2)
    params = pltpu.CompilerParams(
        dimension_semantics=("arbitrary",), vmem_limit_bytes=36 * 1024 * 1024
    )
    score_block = pl.BlockSpec((2 * STEP - 2, cond_rows, lat_rows), lambda i: (i, 0, 0))
    share_block = pl.BlockSpec((dates, lat_rows // dates, STEP * PAIR), lambda i: (0, 0, i))
    sums_block = pl.BlockSpec((dates, STEP, 4, lat_rows), lambda i: (0, i, 0, 0))
    score_shape = pltpu.HBM((2 * (pairs - pairs // STEP), cond_rows, lat_rows), jnp.bfloat16)
    near_shape = pltpu.VMEM((2 * (pairs // STEP), cond_rows, lat_rows), jnp.bfloat16)
    vmem = pl.BlockSpec(memory_space=pltpu.VMEM)
    piece_shape = pltpu.HBM((chips, far, own, cond_rows), jnp.bfloat16)
    weights, carried, near_weights, near_carried, sums, key_raw = pl.pallas_call(
        scores_kernel,
        grid=(pairs // STEP,),
        in_specs=[
            columns(lat_rows),
            columns(lat_rows),
            whole((cond_rows, width)),
            columns(width),
            columns(width),
            whole((1, cond_rows)),
        ],
        out_specs=[score_block, score_block, vmem, vmem, sums_block, columns(cond_rows)],
        out_shape=[
            score_shape,
            score_shape,
            near_shape,
            near_shape,
            pltpu.HBM((dates, pairs, 4, lat_rows), jnp.bfloat16),
            pltpu.HBM((cond_rows, local_width), jnp.float32),
        ],
        scratch_shapes=[pltpu.VMEM((cond_rows, PAIR), jnp.float32)],
        compiler_params=params,
        name="scores",
    )(latent_queries, grad_attention, cond_tokens, w_key, w_value, clear_tokens)
    weights, carried, key_raw = in_hbm(weights, carried, key_raw)
    sums = lax.all_to_all(sums, "date", 0, 0, tiled=True)
    place = jnp.stack([lax.axis_index("x"), lax.axis_index("core"), lax.axis_index("head")])
    grad_q, keep, send = pl.pallas_call(
        grads_kernel,
        grid=(pairs // STEP,),
        in_specs=[
            pl.BlockSpec(memory_space=pltpu.SMEM),
            columns(lat_rows),
            columns(lat_rows),
            columns(cond_rows),
            columns(width),
            columns(width),
            score_block,
            score_block,
            vmem,
            vmem,
            sums_block,
        ],
        out_specs=[share_block, whole(piece_shape.shape), whole(piece_shape.shape)],
        out_shape=[
            pltpu.HBM((dates, lat_rows // dates, local_width), jnp.bfloat16),
            piece_shape,
            piece_shape,
        ],
        scratch_shapes=[pltpu.VMEM((width, cond_rows), jnp.float32)],
        compiler_params=params,
        name="grads",
    )(place, latent_queries, grad_attention, key_raw, w_key, w_value, weights, carried, near_weights, near_carried, sums)
    share_parts = lax.all_to_all(grad_q, "date", 0, 0, tiled=True)
    other = lax.ppermute(send, "core", [(0, 1), (1, 0)])
    halves = lax.optimization_barrier([add(keep[chip], other[chip]) for chip in range(chips)])
    near_parts = halves[:1] + [
        lax.ppermute(halves[chip], CHIPS, [(i, i ^ chip) for i in range(chips)])
        for chip in range(1, chips)
    ]
    near_sum, share_parts = lax.optimization_barrier((add(*near_parts), share_parts))
    far_parts = lax.all_to_all(near_sum, "z", 0, 0, tiled=True)
    grad_queries = jnp.sum(share_parts.astype(jnp.float32), axis=0).astype(jnp.bfloat16)
    grad_cond = jnp.sum(far_parts.astype(jnp.float32), axis=0)
    return (grad_queries, grad_cond.T.astype(jnp.bfloat16))


def solution(mesh):
    space, dates, heads = mesh.devices.shape
    split = Mesh(
        mesh.devices.reshape(space // 4, 2, 2, dates, heads), ("z", "x", "core", "date", "head")
    )
    return jax.shard_map(
        body,
        mesh=split,
        in_specs=(
            P(SPACE, "head"),
            P(SPACE, "head"),
            P("date", None),
            P(None, "head"),
            P(None, "head"),
            P(SPACE, "date"),
        ),
        out_specs=(P(SPACE + ("date",), "head"), P("date", SPACE + ("head",))),
        check_vma=False,
    )
```

```python
import jax
import jax.numpy as jnp
from jax import lax
from jax.experimental import pallas as pl
from jax.experimental.pallas import tpu as pltpu
from jax.sharding import Mesh, PartitionSpec as P

DH = 64
PAIR = 2 * DH
STEP = 3
SPACE = ("z", "x", "core")
CHIPS = ("x", "head")

NORM_EPSILON = 1e-06

NT = (((1,), (1,)), ((), ()))
NN = (((1,), (0,)), ((), ()))


def dot(a, b, dims=NN):
    return lax.dot_general(a, b, dims, preferred_element_type=jnp.float32)


def head_mean(x):
    first = lax.broadcasted_iota(jnp.int32, x.shape, 1) < DH
    zero = jnp.zeros_like(x)
    left = jnp.sum(jnp.where(first, x, zero), axis=1, keepdims=True)
    right = jnp.sum(jnp.where(first, zero, x), axis=1, keepdims=True)
    return jnp.where(first, left, right) * (1.0 / DH)


def place_of(sub, head, w_ref, e_ref, w_near_ref, e_near_ref):
    if sub < STEP - 1:
        return w_ref, e_ref, 2 * sub + head
    return w_near_ref, e_near_ref, 2 * pl.program_id(0) + head


def scores_kernel(
    q_ref, g_ref, cond_ref, wk_ref, wv_ref, clear_ref,
    w_ref, e_ref, w_near_ref, e_near_ref, sums_ref, keys_ref, mask_ref
):
    cond_rows = cond_ref.shape[0]
    lat_rows = q_ref.shape[0]

    @pl.when(pl.program_id(0) == 0)
    def _():
        mask_ref[...] = jnp.broadcast_to(clear_ref[...].astype(jnp.float32), (PAIR, cond_rows)).T

    projected = dot(cond_ref[...], jnp.concatenate([wk_ref[...], wv_ref[...]], axis=1))
    for sub in range(STEP):
        lanes = slice(sub * PAIR, (sub + 1) * PAIR)
        key_raw = projected[:, lanes]
        keys_ref[:, lanes] = key_raw
        key_normed = key_raw * lax.rsqrt(head_mean(key_raw * key_raw) + NORM_EPSILON)
        key_unit = key_normed.astype(jnp.bfloat16)
        values = projected[:, (STEP + sub) * PAIR : (STEP + sub + 1) * PAIR].astype(jnp.bfloat16)
        q = q_ref[:, lanes].astype(jnp.float32)
        q_unit = (q * lax.rsqrt(head_mean(q * q) + NORM_EPSILON)).astype(jnp.bfloat16)
        first = lax.broadcasted_iota(jnp.int32, key_unit.shape, 1) < DH
        nothing = jnp.zeros_like(key_unit)
        mask = jnp.concatenate([mask_ref[...]] * (lat_rows // PAIR), axis=1)
        sums = []
        for head in range(2):
            mine = first if head == 0 else ~first
            scores = dot(jnp.where(mine, key_unit, nothing), q_unit, NT) * (DH ** -0.5)
            dprob = dot(jnp.where(mine, values, nothing), g_ref[:, lanes], NT)
            weights = jnp.exp(scores) * mask
            carried = weights * dprob
            own_w, own_e, at = place_of(sub, head, w_ref, e_ref, w_near_ref, e_near_ref)
            own_w[at] = weights.astype(jnp.bfloat16)
            own_e[at] = carried.astype(jnp.bfloat16)
            sums += [jnp.sum(weights, axis=0, keepdims=True), jnp.sum(carried, axis=0, keepdims=True)]
        sums = jnp.concatenate(sums, axis=0).astype(sums_ref.dtype)
        sums_ref[:, sub] = jnp.broadcast_to(sums[None], (sums_ref.shape[0],) + sums.shape)


def means_of(sums_ref, pair, head):
    sums = jnp.sum(sums_ref[:, pair, 2 * head : 2 * head + 2].astype(jnp.float32), axis=0)
    inverse = 1.0 / sums[:1]
    return inverse, sums[1:] * inverse


def grads_kernel(
    place_ref, q_ref, g_ref, keys_ref, wk_ref, wv_ref, w_ref, e_ref, w_near_ref, e_near_ref, sums_ref,
    gq_ref, keep_ref, send_ref, acc_ref
):
    cond_rows = keys_ref.shape[0]
    step = pl.program_id(0)
    both = []
    rest = []
    for sub in range(STEP):
        lanes = slice(sub * PAIR, (sub + 1) * PAIR)
        q = q_ref[:, lanes].astype(jnp.float32)
        q_factor = lax.rsqrt(head_mean(q * q) + NORM_EPSILON)
        q_normed = q * q_factor
        q_unit = q_normed.astype(jnp.bfloat16)
        key_raw = keys_ref[:, lanes]
        key_factor = lax.rsqrt(head_mean(key_raw * key_raw) + NORM_EPSILON)
        key_normed = key_raw * key_factor
        turned = key_normed.T.astype(jnp.bfloat16)
        probs = []
        dscores = []
        for head in range(2):
            inverse, mean = means_of(sums_ref, sub, head)
            own_w, own_e, at = place_of(sub, head, w_ref, e_ref, w_near_ref, e_near_ref)
            weights = own_w[at].astype(jnp.float32)
            probs.append((weights * inverse).astype(jnp.bfloat16))
            dscore = (own_e[at].astype(jnp.float32) - weights * mean) * inverse
            dscores.append(dscore.astype(jnp.bfloat16))
        rest.append((lanes, turned, dscores, q_factor, q_normed))
        lane = lax.broadcasted_iota(jnp.int32, (cond_rows, PAIR), 1)
        grad_values = dot(jnp.concatenate(probs, axis=0), g_ref[:, lanes])
        grad_keys = dot(jnp.concatenate(dscores, axis=0), q_unit)
        gv = jnp.where(lane < DH, grad_values[:cond_rows], grad_values[cond_rows:])
        gk = jnp.where(lane < DH, grad_keys[:cond_rows], grad_keys[cond_rows:]) * (DH ** -0.5)
        gk_back = key_factor * (gk - key_normed * head_mean(gk * key_normed))
        both += [gk_back.astype(jnp.bfloat16), gv.astype(jnp.bfloat16)]
    for lanes, turned, dscores, q_factor, q_normed in rest:
        gq = [dot(turned[head * DH : (head + 1) * DH], dscores[head]) for head in range(2)]
        gq = jnp.concatenate(gq, axis=0).T * (DH ** -0.5)
        gq = q_factor * (gq - q_normed * head_mean(gq * q_normed))
        gq_ref[:, :, lanes] = gq.astype(gq_ref.dtype).reshape(gq_ref.shape[:2] + (PAIR,))
    w_both = []
    for sub in range(STEP):
        lanes = slice(sub * PAIR, (sub + 1) * PAIR)
        w_both += [wk_ref[:, lanes], wv_ref[:, lanes]]
    part = dot(jnp.concatenate(w_both, axis=1), jnp.concatenate(both, axis=1), NT)

    @pl.when(step == 0)
    def _():
        acc_ref[...] = part

    @pl.when(step > 0)
    def _():
        acc_ref[...] += part

    @pl.when(step == pl.num_programs(0) - 1)
    def _():
        chips, far, own = keep_ref.shape[:3]
        x, core, head = place_ref[0], place_ref[1], place_ref[2]
        for chip in range(chips):
            to_x = x ^ (chip // 2)
            to_head = head ^ (chip % 2)
            for ref, to_core in ((keep_ref, core), (send_ref, core ^ 1)):
                near = (to_x * 2 + to_core) * 2 + to_head
                for i in range(far):
                    start = pl.multiple_of((i * 8 + near) * own, own)
                    ref[chip, i] = acc_ref[pl.ds(start, own), :].astype(ref.dtype)


def columns(rows):
    return pl.BlockSpec((rows, STEP * PAIR), lambda i: (0, i))


def whole(shape):
    return pl.BlockSpec(shape, lambda i: (0,) * len(shape), pipeline_mode=pl.Buffered(1))


def in_hbm(*arrays):
    return [pltpu.with_memory_space_constraint(array, pltpu.HBM) for array in arrays]


def add(*parts):
    return sum(part.astype(jnp.float32) for part in parts).astype(jnp.bfloat16)


def body(latent_queries, grad_attention, cond_tokens, w_key, w_value, clear_tokens):
    lat_rows, local_width = latent_queries.shape
    cond_rows, width = cond_tokens.shape
    pairs = local_width // PAIR
    latent_queries, grad_attention, cond_tokens, w_key, w_value, clear_tokens = in_hbm(
        latent_queries, grad_attention, cond_tokens, w_key, w_value, clear_tokens
    )
    dates = lax.axis_size("date")
    far = lax.axis_size("z")
    chips = lax.axis_size(CHIPS)
    own = width // (far * chips * 2)
    params = pltpu.CompilerParams(
        dimension_semantics=("arbitrary",), vmem_limit_bytes=36 * 1024 * 1024
    )
    score_block = pl.BlockSpec((2 * STEP - 2, cond_rows, lat_rows), lambda i: (i, 0, 0))
    share_block = pl.BlockSpec((dates, lat_rows // dates, STEP * PAIR), lambda i: (0, 0, i))
    sums_block = pl.BlockSpec((dates, STEP, 4, lat_rows), lambda i: (0, i, 0, 0))
    score_shape = pltpu.HBM((2 * (pairs - pairs // STEP), cond_rows, lat_rows), jnp.bfloat16)
    near_shape = pltpu.VMEM((2 * (pairs // STEP), cond_rows, lat_rows), jnp.bfloat16)
    vmem = pl.BlockSpec(memory_space=pltpu.VMEM)
    piece_shape = pltpu.HBM((chips, far, own, cond_rows), jnp.bfloat16)
    weights, carried, near_weights, near_carried, sums, key_raw = pl.pallas_call(
        scores_kernel,
        grid=(pairs // STEP,),
        in_specs=[
            columns(lat_rows),
            columns(lat_rows),
            whole((cond_rows, width)),
            columns(width),
            columns(width),
            whole((1, cond_rows)),
        ],
        out_specs=[score_block, score_block, vmem, vmem, sums_block, columns(cond_rows)],
        out_shape=[
            score_shape,
            score_shape,
            near_shape,
            near_shape,
            pltpu.HBM((dates, pairs, 4, lat_rows), jnp.bfloat16),
            pltpu.HBM((cond_rows, local_width), jnp.float32),
        ],
        scratch_shapes=[pltpu.VMEM((cond_rows, PAIR), jnp.float32)],
        compiler_params=params,
        name="scores",
    )(latent_queries, grad_attention, cond_tokens, w_key, w_value, clear_tokens)
    weights, carried, key_raw = in_hbm(weights, carried, key_raw)
    sums = lax.all_to_all(sums, "date", 0, 0, tiled=True)
    place = jnp.stack([lax.axis_index("x"), lax.axis_index("core"), lax.axis_index("head")])
    grad_q, keep, send = pl.pallas_call(
        grads_kernel,
        grid=(pairs // STEP,),
        in_specs=[
            pl.BlockSpec(memory_space=pltpu.SMEM),
            columns(lat_rows),
            columns(lat_rows),
            columns(cond_rows),
            columns(width),
            columns(width),
            score_block,
            score_block,
            vmem,
            vmem,
            sums_block,
        ],
        out_specs=[share_block, whole(piece_shape.shape), whole(piece_shape.shape)],
        out_shape=[
            pltpu.HBM((dates, lat_rows // dates, local_width), jnp.bfloat16),
            piece_shape,
            piece_shape,
        ],
        scratch_shapes=[pltpu.VMEM((width, cond_rows), jnp.float32)],
        compiler_params=params,
        name="grads",
    )(place, latent_queries, grad_attention, key_raw, w_key, w_value, weights, carried, near_weights, near_carried, sums)
    share_parts = lax.all_to_all(grad_q, "date", 0, 0, tiled=True)
    other = lax.ppermute(send, "core", [(0, 1), (1, 0)])
    halves = lax.optimization_barrier([add(keep[chip], other[chip]) for chip in range(chips)])
    near_parts = halves[:1] + [
        lax.ppermute(halves[chip], CHIPS, [(i, i ^ chip) for i in range(chips)])
        for chip in range(1, chips)
    ]
    near_sum, share_parts = lax.optimization_barrier((add(*near_parts), share_parts))
    far_parts = lax.all_to_all(near_sum, "z", 0, 0, tiled=True)
    grad_queries = jnp.sum(share_parts.astype(jnp.float32), axis=0).astype(jnp.bfloat16)
    grad_cond = jnp.sum(far_parts.astype(jnp.float32), axis=0)
    return (grad_queries, grad_cond.T.astype(jnp.bfloat16))


def solution(mesh):
    space, dates, heads = mesh.devices.shape
    split = Mesh(
        mesh.devices.reshape(space // 4, 2, 2, dates, heads), ("z", "x", "core", "date", "head")
    )
    return jax.shard_map(
        body,
        mesh=split,
        in_specs=(
            P(SPACE, "head"),
            P(SPACE, "head"),
            P("date", None),
            P(None, "head"),
            P(None, "head"),
            P(SPACE, "date"),
        ),
        out_specs=(P(SPACE + ("date",), "head"), P("date", SPACE + ("head",))),
        check_vma=False,
    )
```

```python
import jax
import jax.numpy as jnp
from jax import lax
from jax.experimental import pallas as pl
from jax.experimental.pallas import tpu as pltpu
from jax.sharding import Mesh, PartitionSpec as P

DH = 64
PAIR = 2 * DH
STEP = 3
SPACE = ("z", "x", "core")
CHIPS = ("x", "head")

NORM_EPSILON = 1e-06

NT = (((1,), (1,)), ((), ()))
NN = (((1,), (0,)), ((), ()))


def dot(a, b, dims=NN):
    return lax.dot_general(a, b, dims, preferred_element_type=jnp.float32)


def head_mean(x):
    first = lax.broadcasted_iota(jnp.int32, x.shape, 1) < DH
    zero = jnp.zeros_like(x)
    left = jnp.sum(jnp.where(first, x, zero), axis=1, keepdims=True)
    right = jnp.sum(jnp.where(first, zero, x), axis=1, keepdims=True)
    return jnp.where(first, left, right) * (1.0 / DH)


def place_of(sub, head, w_ref, e_ref, w_near_ref, e_near_ref):
    if sub < STEP - 1:
        return w_ref, e_ref, 2 * sub + head
    return w_near_ref, e_near_ref, 2 * pl.program_id(0) + head


def scores_kernel(
    q_ref, g_ref, cond_ref, wk_ref, wv_ref, clear_ref,
    w_ref, e_ref, w_near_ref, e_near_ref, sums_ref, keys_ref, mask_ref
):
    cond_rows = cond_ref.shape[0]
    lat_rows = q_ref.shape[0]

    @pl.when(pl.program_id(0) == 0)
    def _():
        mask_ref[...] = jnp.broadcast_to(clear_ref[...].astype(jnp.float32), (PAIR, cond_rows)).T

    projected = dot(cond_ref[...], jnp.concatenate([wk_ref[...], wv_ref[...]], axis=1))
    for sub in range(STEP):
        lanes = slice(sub * PAIR, (sub + 1) * PAIR)
        key_raw = projected[:, lanes]
        keys_ref[:, lanes] = key_raw
        key_normed = key_raw * lax.rsqrt(head_mean(key_raw * key_raw) + NORM_EPSILON)
        key_unit = key_normed.astype(jnp.bfloat16)
        values = projected[:, (STEP + sub) * PAIR : (STEP + sub + 1) * PAIR].astype(jnp.bfloat16)
        q = q_ref[:, lanes].astype(jnp.float32)
        q_unit = (q * lax.rsqrt(head_mean(q * q) + NORM_EPSILON)).astype(jnp.bfloat16)
        first = lax.broadcasted_iota(jnp.int32, key_unit.shape, 1) < DH
        nothing = jnp.zeros_like(key_unit)
        mask = jnp.concatenate([mask_ref[...]] * (lat_rows // PAIR), axis=1)
        sums = []
        for head in range(2):
            mine = first if head == 0 else ~first
            scores = dot(jnp.where(mine, key_unit, nothing), q_unit, NT) * (DH ** -0.5)
            dprob = dot(jnp.where(mine, values, nothing), g_ref[:, lanes], NT)
            weights = jnp.exp(scores) * mask
            carried = weights * dprob
            own_w, own_e, at = place_of(sub, head, w_ref, e_ref, w_near_ref, e_near_ref)
            own_w[at] = weights.astype(jnp.bfloat16)
            own_e[at] = carried.astype(jnp.bfloat16)
            sums += [jnp.sum(weights, axis=0, keepdims=True), jnp.sum(carried, axis=0, keepdims=True)]
        sums = jnp.concatenate(sums, axis=0).astype(sums_ref.dtype)
        sums_ref[:, sub] = jnp.broadcast_to(sums[None], (sums_ref.shape[0],) + sums.shape)


def means_of(sums_ref, pair, head):
    sums = jnp.sum(sums_ref[:, pair, 2 * head : 2 * head + 2].astype(jnp.float32), axis=0)
    inverse = 1.0 / sums[:1]
    return inverse, sums[1:] * inverse


def grads_kernel(
    place_ref, q_ref, g_ref, keys_ref, wk_ref, wv_ref, w_ref, e_ref, w_near_ref, e_near_ref, sums_ref,
    gq_ref, keep_ref, send_ref, acc_ref
):
    cond_rows = keys_ref.shape[0]
    step = pl.program_id(0)
    both = []
    rest = []
    for sub in range(STEP):
        lanes = slice(sub * PAIR, (sub + 1) * PAIR)
        q = q_ref[:, lanes].astype(jnp.float32)
        q_factor = lax.rsqrt(head_mean(q * q) + NORM_EPSILON)
        q_normed = q * q_factor
        q_unit = q_normed.astype(jnp.bfloat16)
        key_raw = keys_ref[:, lanes]
        key_factor = lax.rsqrt(head_mean(key_raw * key_raw) + NORM_EPSILON)
        key_normed = key_raw * key_factor
        turned = key_normed.T.astype(jnp.bfloat16)
        probs = []
        dscores = []
        for head in range(2):
            inverse, mean = means_of(sums_ref, sub, head)
            own_w, own_e, at = place_of(sub, head, w_ref, e_ref, w_near_ref, e_near_ref)
            weights = own_w[at].astype(jnp.float32)
            probs.append((weights * inverse).astype(jnp.bfloat16))
            dscore = (own_e[at].astype(jnp.float32) - weights * mean) * inverse
            dscores.append(dscore.astype(jnp.bfloat16))
        rest.append((lanes, turned, dscores, q_factor, q_normed))
        lane = lax.broadcasted_iota(jnp.int32, (cond_rows, PAIR), 1)
        grad_values = dot(jnp.concatenate(probs, axis=0), g_ref[:, lanes])
        grad_keys = dot(jnp.concatenate(dscores, axis=0), q_unit)
        gv = jnp.where(lane < DH, grad_values[:cond_rows], grad_values[cond_rows:])
        gk = jnp.where(lane < DH, grad_keys[:cond_rows], grad_keys[cond_rows:]) * (DH ** -0.5)
        gk_back = key_factor * (gk - key_normed * head_mean(gk * key_normed))
        both += [gk_back.astype(jnp.bfloat16), gv.astype(jnp.bfloat16)]
    for lanes, turned, dscores, q_factor, q_normed in rest:
        gq = [dot(turned[head * DH : (head + 1) * DH], dscores[head]) for head in range(2)]
        gq = jnp.concatenate(gq, axis=0).T * (DH ** -0.5)
        gq = q_factor * (gq - q_normed * head_mean(gq * q_normed))
        gq_ref[:, :, lanes] = gq.astype(gq_ref.dtype).reshape(gq_ref.shape[:2] + (PAIR,))
    w_both = []
    for sub in range(STEP):
        lanes = slice(sub * PAIR, (sub + 1) * PAIR)
        w_both += [wk_ref[:, lanes], wv_ref[:, lanes]]
    part = dot(jnp.concatenate(w_both, axis=1), jnp.concatenate(both, axis=1), NT)

    @pl.when(step == 0)
    def _():
        acc_ref[...] = part

    @pl.when(step > 0)
    def _():
        acc_ref[...] += part

    @pl.when(step == pl.num_programs(0) - 1)
    def _():
        chips, far, own = keep_ref.shape[:3]
        x, core, head = place_ref[0], place_ref[1], place_ref[2]
        for chip in range(chips):
            to_x = x ^ (chip // 2)
            to_head = head ^ (chip % 2)
            for ref, to_core in ((keep_ref, core), (send_ref, core ^ 1)):
                near = (to_x * 2 + to_core) * 2 + to_head
                for i in range(far):
                    start = pl.multiple_of((i * 8 + near) * own, own)
                    ref[chip, i] = acc_ref[pl.ds(start, own), :].astype(ref.dtype)


def columns(rows):
    return pl.BlockSpec((rows, STEP * PAIR), lambda i: (0, i))


def whole(shape):
    return pl.BlockSpec(shape, lambda i: (0,) * len(shape), pipeline_mode=pl.Buffered(1))


def in_hbm(*arrays):
    return [pltpu.with_memory_space_constraint(array, pltpu.HBM) for array in arrays]


def add(*parts):
    return sum(part.astype(jnp.float32) for part in parts).astype(jnp.bfloat16)


def body(latent_queries, grad_attention, cond_tokens, w_key, w_value, clear_tokens):
    lat_rows, local_width = latent_queries.shape
    cond_rows, width = cond_tokens.shape
    pairs = local_width // PAIR
    latent_queries, grad_attention, cond_tokens, w_key, w_value, clear_tokens = in_hbm(
        latent_queries, grad_attention, cond_tokens, w_key, w_value, clear_tokens
    )
    dates = lax.axis_size("date")
    far = lax.axis_size("z")
    chips = lax.axis_size(CHIPS)
    own = width // (far * chips * 2)
    params = pltpu.CompilerParams(
        dimension_semantics=("arbitrary",), vmem_limit_bytes=36 * 1024 * 1024
    )
    score_block = pl.BlockSpec((2 * STEP - 2, cond_rows, lat_rows), lambda i: (i, 0, 0))
    share_block = pl.BlockSpec((dates, lat_rows // dates, STEP * PAIR), lambda i: (0, 0, i))
    sums_block = pl.BlockSpec((dates, STEP, 4, lat_rows), lambda i: (0, i, 0, 0))
    score_shape = pltpu.HBM((2 * (pairs - pairs // STEP), cond_rows, lat_rows), jnp.bfloat16)
    near_shape = pltpu.VMEM((2 * (pairs // STEP), cond_rows, lat_rows), jnp.bfloat16)
    vmem = pl.BlockSpec(memory_space=pltpu.VMEM)
    piece_shape = pltpu.HBM((chips, far, own, cond_rows), jnp.bfloat16)
    weights, carried, near_weights, near_carried, sums, key_raw = pl.pallas_call(
        scores_kernel,
        grid=(pairs // STEP,),
        in_specs=[
            columns(lat_rows),
            columns(lat_rows),
            whole((cond_rows, width)),
            columns(width),
            columns(width),
            whole((1, cond_rows)),
        ],
        out_specs=[score_block, score_block, vmem, vmem, sums_block, columns(cond_rows)],
        out_shape=[
            score_shape,
            score_shape,
            near_shape,
            near_shape,
            pltpu.HBM((dates, pairs, 4, lat_rows), jnp.bfloat16),
            pltpu.HBM((cond_rows, local_width), jnp.float32),
        ],
        scratch_shapes=[pltpu.VMEM((cond_rows, PAIR), jnp.float32)],
        compiler_params=params,
        name="scores",
    )(latent_queries, grad_attention, cond_tokens, w_key, w_value, clear_tokens)
    weights, carried, key_raw = in_hbm(weights, carried, key_raw)
    sums = lax.all_to_all(sums, "date", 0, 0, tiled=True)
    place = jnp.stack([lax.axis_index("x"), lax.axis_index("core"), lax.axis_index("head")])
    grad_q, keep, send = pl.pallas_call(
        grads_kernel,
        grid=(pairs // STEP,),
        in_specs=[
            pl.BlockSpec(memory_space=pltpu.SMEM),
            columns(lat_rows),
            columns(lat_rows),
            columns(cond_rows),
            columns(width),
            columns(width),
            score_block,
            score_block,
            vmem,
            vmem,
            sums_block,
        ],
        out_specs=[share_block, whole(piece_shape.shape), whole(piece_shape.shape)],
        out_shape=[
            pltpu.HBM((dates, lat_rows // dates, local_width), jnp.bfloat16),
            piece_shape,
            piece_shape,
        ],
        scratch_shapes=[pltpu.VMEM((width, cond_rows), jnp.float32)],
        compiler_params=params,
        name="grads",
    )(place, latent_queries, grad_attention, key_raw, w_key, w_value, weights, carried, near_weights, near_carried, sums)
    grad_q, stays = lax.optimization_barrier((grad_q, keep[0]))
    share_parts = lax.all_to_all(grad_q, "date", 0, 0, tiled=True)
    other = lax.ppermute(send, "core", [(0, 1), (1, 0)])
    halves = lax.optimization_barrier(
        [add(stays, other[0])] + [add(keep[chip], other[chip]) for chip in range(1, chips)]
    )
    near_parts = halves[:1] + [
        lax.ppermute(halves[chip], CHIPS, [(i, i ^ chip) for i in range(chips)])
        for chip in range(1, chips)
    ]
    near_sum, share_parts = lax.optimization_barrier((add(*near_parts), share_parts))
    far_parts = lax.all_to_all(near_sum, "z", 0, 0, tiled=True)
    grad_queries = jnp.sum(share_parts.astype(jnp.float32), axis=0).astype(jnp.bfloat16)
    grad_cond = jnp.sum(far_parts.astype(jnp.float32), axis=0)
    return (grad_queries, grad_cond.T.astype(jnp.bfloat16))


def solution(mesh):
    space, dates, heads = mesh.devices.shape
    split = Mesh(
        mesh.devices.reshape(space // 4, 2, 2, dates, heads), ("z", "x", "core", "date", "head")
    )
    return jax.shard_map(
        body,
        mesh=split,
        in_specs=(
            P(SPACE, "head"),
            P(SPACE, "head"),
            P("date", None),
            P(None, "head"),
            P(None, "head"),
            P(SPACE, "date"),
        ),
        out_specs=(P(SPACE + ("date",), "head"), P("date", SPACE + ("head",))),
        check_vma=False,
    )
```

```python
import jax
import jax.numpy as jnp
from jax import lax
from jax.experimental import pallas as pl
from jax.experimental.pallas import tpu as pltpu
from jax.sharding import Mesh, PartitionSpec as P

DH = 64
PAIR = 2 * DH
STEP = 3
SPACE = ("z", "x", "core")
CHIPS = ("x", "head")

NORM_EPSILON = 1e-06

NT = (((1,), (1,)), ((), ()))
NN = (((1,), (0,)), ((), ()))


def dot(a, b, dims=NN):
    return lax.dot_general(a, b, dims, preferred_element_type=jnp.float32)


def head_mean(x):
    first = lax.broadcasted_iota(jnp.int32, x.shape, 1) < DH
    zero = jnp.zeros_like(x)
    left = jnp.sum(jnp.where(first, x, zero), axis=1, keepdims=True)
    right = jnp.sum(jnp.where(first, zero, x), axis=1, keepdims=True)
    return jnp.where(first, left, right) * (1.0 / DH)


def place_of(sub, head, w_ref, e_ref, w_near_ref, e_near_ref):
    if sub < STEP - 1:
        return w_ref, e_ref, 2 * sub + head
    return w_near_ref, e_near_ref, 2 * pl.program_id(0) + head


def scores_kernel(
    q_ref, g_ref, cond_ref, wk_ref, wv_ref, clear_ref,
    w_ref, e_ref, w_near_ref, e_near_ref, sums_ref, keys_ref, mask_ref
):
    cond_rows = cond_ref.shape[0]
    lat_rows = q_ref.shape[0]

    @pl.when(pl.program_id(0) == 0)
    def _():
        mask_ref[...] = jnp.broadcast_to(clear_ref[...].astype(jnp.float32), (PAIR, cond_rows)).T

    projected = dot(cond_ref[...], jnp.concatenate([wk_ref[...], wv_ref[...]], axis=1))
    for sub in range(STEP):
        lanes = slice(sub * PAIR, (sub + 1) * PAIR)
        key_raw = projected[:, lanes]
        keys_ref[:, lanes] = key_raw
        key_normed = key_raw * lax.rsqrt(head_mean(key_raw * key_raw) + NORM_EPSILON)
        key_unit = key_normed.astype(jnp.bfloat16)
        values = projected[:, (STEP + sub) * PAIR : (STEP + sub + 1) * PAIR].astype(jnp.bfloat16)
        q = q_ref[:, lanes].astype(jnp.float32)
        q_unit = (q * lax.rsqrt(head_mean(q * q) + NORM_EPSILON)).astype(jnp.bfloat16)
        first = lax.broadcasted_iota(jnp.int32, key_unit.shape, 1) < DH
        nothing = jnp.zeros_like(key_unit)
        mask = jnp.concatenate([mask_ref[...]] * (lat_rows // PAIR), axis=1)
        sums = []
        for head in range(2):
            mine = first if head == 0 else ~first
            scores = dot(jnp.where(mine, key_unit, nothing), q_unit, NT) * (DH ** -0.5)
            dprob = dot(jnp.where(mine, values, nothing), g_ref[:, lanes], NT)
            weights = jnp.exp(scores) * mask
            carried = weights * dprob
            own_w, own_e, at = place_of(sub, head, w_ref, e_ref, w_near_ref, e_near_ref)
            own_w[at] = weights.astype(jnp.bfloat16)
            own_e[at] = carried.astype(jnp.bfloat16)
            sums += [jnp.sum(weights, axis=0, keepdims=True), jnp.sum(carried, axis=0, keepdims=True)]
        sums = jnp.concatenate(sums, axis=0).astype(sums_ref.dtype)
        sums_ref[:, sub] = jnp.broadcast_to(sums[None], (sums_ref.shape[0],) + sums.shape)


def means_of(sums_ref, pair, head):
    sums = jnp.sum(sums_ref[:, pair, 2 * head : 2 * head + 2].astype(jnp.float32), axis=0)
    inverse = 1.0 / sums[:1]
    return inverse, sums[1:] * inverse


def grads_kernel(
    place_ref, q_ref, g_ref, keys_ref, wk_ref, wv_ref, w_ref, e_ref, w_near_ref, e_near_ref, sums_ref,
    gq_ref, keep_ref, send_ref, acc_ref
):
    cond_rows = keys_ref.shape[0]
    step = pl.program_id(0)
    both = []
    rest = []
    for sub in range(STEP):
        lanes = slice(sub * PAIR, (sub + 1) * PAIR)
        q = q_ref[:, lanes].astype(jnp.float32)
        q_factor = lax.rsqrt(head_mean(q * q) + NORM_EPSILON)
        q_normed = q * q_factor
        q_unit = q_normed.astype(jnp.bfloat16)
        key_raw = keys_ref[:, lanes]
        key_factor = lax.rsqrt(head_mean(key_raw * key_raw) + NORM_EPSILON)
        key_normed = key_raw * key_factor
        turned = key_normed.astype(jnp.bfloat16).T
        probs = []
        dscores = []
        for head in range(2):
            inverse, mean = means_of(sums_ref, sub, head)
            own_w, own_e, at = place_of(sub, head, w_ref, e_ref, w_near_ref, e_near_ref)
            weights = own_w[at].astype(jnp.float32)
            probs.append((weights * inverse).astype(jnp.bfloat16))
            dscore = (own_e[at].astype(jnp.float32) - weights * mean) * inverse
            dscores.append(dscore.astype(jnp.bfloat16))
        rest.append((lanes, turned, dscores, q_factor, q_normed))
        lane = lax.broadcasted_iota(jnp.int32, (cond_rows, PAIR), 1)
        grad_values = dot(jnp.concatenate(probs, axis=0), g_ref[:, lanes])
        grad_keys = dot(jnp.concatenate(dscores, axis=0), q_unit)
        gv = jnp.where(lane < DH, grad_values[:cond_rows], grad_values[cond_rows:])
        gk = jnp.where(lane < DH, grad_keys[:cond_rows], grad_keys[cond_rows:]) * (DH ** -0.5)
        gk_back = key_factor * (gk - key_normed * head_mean(gk * key_normed))
        both += [gk_back.astype(jnp.bfloat16), gv.astype(jnp.bfloat16)]
    for lanes, turned, dscores, q_factor, q_normed in rest:
        gq = [dot(turned[head * DH : (head + 1) * DH], dscores[head]) for head in range(2)]
        gq = jnp.concatenate(gq, axis=0).T * (DH ** -0.5)
        gq = q_factor * (gq - q_normed * head_mean(gq * q_normed))
        gq_ref[:, :, lanes] = gq.astype(gq_ref.dtype).reshape(gq_ref.shape[:2] + (PAIR,))
    w_both = []
    for sub in range(STEP):
        lanes = slice(sub * PAIR, (sub + 1) * PAIR)
        w_both += [wk_ref[:, lanes], wv_ref[:, lanes]]
    part = dot(jnp.concatenate(w_both, axis=1), jnp.concatenate(both, axis=1), NT)

    @pl.when(step == 0)
    def _():
        acc_ref[...] = part

    @pl.when(step > 0)
    def _():
        acc_ref[...] += part

    @pl.when(step == pl.num_programs(0) - 1)
    def _():
        chips, far, own = keep_ref.shape[:3]
        x, core, head = place_ref[0], place_ref[1], place_ref[2]
        for chip in range(chips):
            to_x = x ^ (chip // 2)
            to_head = head ^ (chip % 2)
            for ref, to_core in ((keep_ref, core), (send_ref, core ^ 1)):
                near = (to_x * 2 + to_core) * 2 + to_head
                for i in range(far):
                    start = pl.multiple_of((i * 8 + near) * own, own)
                    ref[chip, i] = acc_ref[pl.ds(start, own), :].astype(ref.dtype)


def columns(rows):
    return pl.BlockSpec((rows, STEP * PAIR), lambda i: (0, i))


def whole(shape):
    return pl.BlockSpec(shape, lambda i: (0,) * len(shape), pipeline_mode=pl.Buffered(1))


def in_hbm(*arrays):
    return [pltpu.with_memory_space_constraint(array, pltpu.HBM) for array in arrays]


def add(*parts):
    return sum(part.astype(jnp.float32) for part in parts).astype(jnp.bfloat16)


def body(latent_queries, grad_attention, cond_tokens, w_key, w_value, clear_tokens):
    lat_rows, local_width = latent_queries.shape
    cond_rows, width = cond_tokens.shape
    pairs = local_width // PAIR
    latent_queries, grad_attention, cond_tokens, w_key, w_value, clear_tokens = in_hbm(
        latent_queries, grad_attention, cond_tokens, w_key, w_value, clear_tokens
    )
    dates = lax.axis_size("date")
    far = lax.axis_size("z")
    chips = lax.axis_size(CHIPS)
    own = width // (far * chips * 2)
    params = pltpu.CompilerParams(
        dimension_semantics=("arbitrary",), vmem_limit_bytes=36 * 1024 * 1024
    )
    score_block = pl.BlockSpec((2 * STEP - 2, cond_rows, lat_rows), lambda i: (i, 0, 0))
    share_block = pl.BlockSpec((dates, lat_rows // dates, STEP * PAIR), lambda i: (0, 0, i))
    sums_block = pl.BlockSpec((dates, STEP, 4, lat_rows), lambda i: (0, i, 0, 0))
    score_shape = pltpu.HBM((2 * (pairs - pairs // STEP), cond_rows, lat_rows), jnp.bfloat16)
    near_shape = pltpu.VMEM((2 * (pairs // STEP), cond_rows, lat_rows), jnp.bfloat16)
    vmem = pl.BlockSpec(memory_space=pltpu.VMEM)
    piece_shape = pltpu.HBM((chips, far, own, cond_rows), jnp.bfloat16)
    weights, carried, near_weights, near_carried, sums, key_raw = pl.pallas_call(
        scores_kernel,
        grid=(pairs // STEP,),
        in_specs=[
            columns(lat_rows),
            columns(lat_rows),
            whole((cond_rows, width)),
            columns(width),
            columns(width),
            whole((1, cond_rows)),
        ],
        out_specs=[score_block, score_block, vmem, vmem, sums_block, columns(cond_rows)],
        out_shape=[
            score_shape,
            score_shape,
            near_shape,
            near_shape,
            pltpu.HBM((dates, pairs, 4, lat_rows), jnp.bfloat16),
            pltpu.HBM((cond_rows, local_width), jnp.float32),
        ],
        scratch_shapes=[pltpu.VMEM((cond_rows, PAIR), jnp.float32)],
        compiler_params=params,
        name="scores",
    )(latent_queries, grad_attention, cond_tokens, w_key, w_value, clear_tokens)
    weights, carried, key_raw = in_hbm(weights, carried, key_raw)
    sums = lax.all_to_all(sums, "date", 0, 0, tiled=True)
    place = jnp.stack([lax.axis_index("x"), lax.axis_index("core"), lax.axis_index("head")])
    grad_q, keep, send = pl.pallas_call(
        grads_kernel,
        grid=(pairs // STEP,),
        in_specs=[
            pl.BlockSpec(memory_space=pltpu.SMEM),
            columns(lat_rows),
            columns(lat_rows),
            columns(cond_rows),
            columns(width),
            columns(width),
            score_block,
            score_block,
            vmem,
            vmem,
            sums_block,
        ],
        out_specs=[share_block, whole(piece_shape.shape), whole(piece_shape.shape)],
        out_shape=[
            pltpu.HBM((dates, lat_rows // dates, local_width), jnp.bfloat16),
            piece_shape,
            piece_shape,
        ],
        scratch_shapes=[pltpu.VMEM((width, cond_rows), jnp.float32)],
        compiler_params=params,
        name="grads",
    )(place, latent_queries, grad_attention, key_raw, w_key, w_value, weights, carried, near_weights, near_carried, sums)
    share_parts = lax.all_to_all(grad_q, "date", 0, 0, tiled=True)
    other = lax.ppermute(send, "core", [(0, 1), (1, 0)])
    halves = lax.optimization_barrier([add(keep[chip], other[chip]) for chip in range(chips)])
    near_parts = halves[:1] + [
        lax.ppermute(halves[chip], CHIPS, [(i, i ^ chip) for i in range(chips)])
        for chip in range(1, chips)
    ]
    near_sum, share_parts = lax.optimization_barrier((add(*near_parts), share_parts))
    far_parts = lax.all_to_all(near_sum, "z", 0, 0, tiled=True)
    grad_queries = jnp.sum(share_parts.astype(jnp.float32), axis=0).astype(jnp.bfloat16)
    grad_cond = jnp.sum(far_parts.astype(jnp.float32), axis=0)
    return (grad_queries, grad_cond.T.astype(jnp.bfloat16))


def solution(mesh):
    space, dates, heads = mesh.devices.shape
    split = Mesh(
        mesh.devices.reshape(space // 4, 2, 2, dates, heads), ("z", "x", "core", "date", "head")
    )
    return jax.shard_map(
        body,
        mesh=split,
        in_specs=(
            P(SPACE, "head"),
            P(SPACE, "head"),
            P("date", None),
            P(None, "head"),
            P(None, "head"),
            P(SPACE, "date"),
        ),
        out_specs=(P(SPACE + ("date",), "head"), P("date", SPACE + ("head",))),
        check_vma=False,
    )
```
